32 devices in a mesh: row: 8 (over z, x), col: 4 (over y, core).
Axes of the slice: x: 2, y: 2, z: 4, core: 2. Of those that a mesh axis runs over, the one named last changes fastest.
Arguments:
- right_side: float32 [384, 8192], P(None, ('row', 'col')), may hold values from -51 to 51
- leaf_inverse: float32 [32, 256, 256], P(('row', 'col')), may hold values from -0.375 to 0.375
- leaf_diag: float32 [32, 256, 256], P(('row', 'col')), may hold values from -0.375 to 0.375
- node_block: float32 [32, 256, 256], P(('row', 'col')), may hold values from -0.375 to 0.375
Outputs:
- solution: float32 [384, 8192], P(None, ('row', 'col'))
- residual_norm: float32 [384], replicated
The draws below stay inside these ranges and needn't reach their ends.
All inputs are finite; a program needn't handle non-finite values.
Results may differ from the reference program's by a relative error of at most 0.0001.
Values sent between devices are 32-bit elements; how exact they have to be, the bound alone decides.
A program may use at most 64 MiB of HBM per device.

```python
import jax
import jax.numpy as jnp
from jax import lax

LEAF = 256
NRHS = 384
NLEAF = 32
N = 8192
DEVICES = 32


def draw_right_side(key, part):
    key_values = jax.random.fold_in(jax.random.fold_in(key, 11), 0)
    rising = 1.0 + 2.0 * jnp.arange(N, dtype=jnp.float32) / (N - 1)
    values = jnp.clip(jax.random.normal(key_values, (NRHS, N), jnp.float32), -5.0, 5.0)
    return values * rising[None, :]


def steps_of(rng, shape, cuts, low, largest):
    level = 1.0
    for dim, parts in cuts:
        steps = jax.random.uniform(jax.random.fold_in(jax.random.fold_in(rng, 6), dim), (parts,), jnp.float32, low / len(cuts), largest / len(cuts))
        level = level * jnp.repeat(jnp.exp(steps), shape[dim] // parts).reshape((-1,) + (1,) * (len(shape) - 1 - dim))
    return level


def noise(own_key, extent, deviation, bound, cuts=(), kind=jnp.bfloat16):
    entries = jax.random.normal(own_key, extent, jnp.float32) * deviation
    if len(cuts) > 0:
        entries = steps_of(own_key, extent, cuts, -0.22, 0.18) * entries
    return jnp.clip(entries, min=-bound, max=bound).astype(kind)


def setup_inputs(seed: int = 0) -> dict:
    splits = jax.random.split(jax.random.key(seed), 5)
    return {
        "right_side": draw_right_side(jax.random.fold_in(splits[4], 71), 0),
        "leaf_inverse": noise(splits[1], (NLEAF, LEAF, LEAF), LEAF ** -0.5, 0.375, ((0, 32),), jnp.float32),
        "leaf_diag": noise(splits[2], (NLEAF, LEAF, LEAF), LEAF ** -0.5, 0.375, ((0, 32),), jnp.float32),
        "node_block": noise(splits[3], (DEVICES, LEAF, LEAF), LEAF ** -0.5, 0.375, ((0, 32),), jnp.float32),
    }


PRECISE = lax.Precision.HIGHEST

def forward(vectors, blocks):
    return jnp.einsum('ncl,nml->ncm', vectors, blocks, precision=PRECISE)

def backward(vectors, blocks):
    return jnp.einsum('ncm,nml->ncl', vectors, blocks, precision=PRECISE)

def reference(right_side, leaf_inverse, leaf_diag, node_block):
    leaf_count = leaf_inverse.shape[0]
    leaf_width = leaf_inverse.shape[1]
    half_width = leaf_width // 2
    rhs_count = right_side.shape[0]
    tree_depth = leaf_count.bit_length() - 1
    leaf_rhs = right_side.reshape(rhs_count, leaf_count, leaf_width).transpose(1, 0, 2)
    lifted = forward(leaf_rhs, leaf_inverse)
    leaf_part = lifted[..., :half_width]
    skeleton = lifted[..., half_width:]
    stored = []
    merged = lifted
    for tree_level in range(1, tree_depth + 1):
        node_count = leaf_count >> tree_level
        paired = skeleton.reshape(node_count, 2, rhs_count, half_width)
        joined = jnp.concatenate([paired[:, 0], paired[:, 1]], axis=-1)
        slot_index = jnp.arange(node_count, dtype=jnp.int32) * 2 ** tree_level + 2 ** (tree_level - 1)
        blocks = node_block[slot_index]
        merged = forward(joined, blocks)
        stored.append((merged[..., :half_width], blocks))
        skeleton = merged[..., half_width:]
    root_solved = forward(merged, node_block[0:1])
    known = jnp.stack([root_solved[0, :, :half_width], root_solved[0, :, half_width:]])
    for tree_level in range(tree_depth - 1, 0, -1):
        eliminated, blocks = stored[tree_level - 1]
        expanded = backward(jnp.concatenate([eliminated, known], axis=-1), blocks)
        node_count = expanded.shape[0]
        known = expanded.reshape(node_count, rhs_count, 2, half_width).transpose(0, 2, 1, 3)
        known = known.reshape(2 * node_count, rhs_count, half_width)
    solved = backward(jnp.concatenate([leaf_part, known], axis=-1), leaf_inverse)
    solution = solved.transpose(1, 0, 2).reshape(rhs_count, leaf_count * leaf_width)
    residual = leaf_rhs - forward(solved, leaf_diag)
    mean_square = lax.optimization_barrier(jnp.sum(residual * residual, axis=(0, 2))) / (leaf_count * leaf_width)
    return (solution, jnp.sqrt(mean_square + 1e-06))
```

```python
import functools

import jax
import jax.numpy as jnp
from jax import lax
from jax.experimental import pallas as pl
from jax.experimental.pallas import tpu as pltpu
from jax.sharding import PartitionSpec as P

MESH = pl.DeviceIdType.MESH
CHUNKS = 2
GROUP_BITS = 3


def halves(value):
    high = value.astype(jnp.bfloat16)
    low = (value - high.astype(jnp.float32)).astype(jnp.bfloat16)
    return high, low


def product(vectors, block, contract):
    rows = vectors.shape[0]
    high, low = halves(vectors)
    block_high, block_low = halves(block)
    dims = (((1,), (contract,)), ((), ()))
    both = lax.dot_general(
        jnp.concatenate([high, low], axis=0), block_high, dims, preferred_element_type=jnp.float32
    )
    cross = lax.dot_general(high, block_low, dims, preferred_element_type=jnp.float32)
    return both[:rows] + (both[rows:] + cross)


def apply_block(vectors, block):
    return product(vectors, block, 1)


def apply_transpose(vectors, block):
    return product(vectors, block, 0)


def kernel(devices, columns, sharded, *refs):
    depth = devices.bit_length() - 1
    (rhs_hbm, leaf_hbm, diag_hbm, node_hbm, out_hbm, norm_ref) = refs[:6]
    (rhs, leaf, diag, solved, blocks, leaf_e, parts, sums) = refs[6:14]
    rest = list(refs[14:])
    skeletons = [rest.pop(0) for _ in range(depth)]
    arrived = [None] + [rest.pop(0) for _ in range(depth)]
    stored = [None] + [rest.pop(0) for _ in range(depth - 1)]
    known_rows = [rest.pop(0) for _ in range(sharded)]
    outgoing = [None] + [rest.pop(0) for _ in range(sharded)]
    (local, block_send, block_recv, up_send, up_recv, down_send, down_recv, sum_send, sum_recv) = rest

    total_rows, width = rhs.shape
    half = width // 2
    chunk = width // CHUNKS
    me = lax.axis_index("row") * columns + lax.axis_index("col")

    def bit(position):
        return lax.rem(lax.div(me, 2**position), 2)

    def place(index):
        return (lax.div(index, columns), lax.rem(index, columns))

    def flipped(delta):
        other = me
        for position in range(depth):
            if delta >> position & 1:
                other = other + (1 - 2 * bit(position)) * 2**position
        return place(other)

    groups = []
    for first in range(0, depth, GROUP_BITS):
        groups.append((first, min(GROUP_BITS, depth - first)))
    deltas = [(g, d, d << first) for g, (first, size) in enumerate(groups) for d in range(1, 2**size)]

    slot = jnp.int32(0)
    for position in range(depth):
        slot = jnp.where(lax.rem(me, 2 ** (position + 1)) == 2**position, position + 1, slot)
    load_node = pltpu.make_async_copy(node_hbm.at[0], blocks.at[slot], local.at[0])
    load_leaf = pltpu.make_async_copy(leaf_hbm.at[0], leaf, local.at[1])
    load_rhs = pltpu.make_async_copy(rhs_hbm, rhs, local.at[2])
    load_diag = pltpu.make_async_copy(diag_hbm.at[0], diag, local.at[3])
    load_node.start()
    load_leaf.start()
    load_rhs.start()
    load_diag.start()

    barrier = pltpu.get_barrier_semaphore()
    for _, _, delta in deltas:
        pl.semaphore_signal(barrier, inc=1, device_id=flipped(delta), device_id_type=MESH)

    def sends(level, position):
        if level == 0:
            return me == 0
        if position == level - 1:
            return lax.rem(me, 2**level) == 2 ** (level - 1)
        return lax.rem(me, 2 ** (position + 1)) == 0

    def receives(level, position):
        if level == 0:
            return me == devices // 2
        if position == level - 1:
            return lax.rem(me, 2**level) == 0
        return lax.rem(me, 2 ** (position + 1)) == 2**position

    def block_copy(level, position, piece):
        return pltpu.make_async_remote_copy(
            src_ref=blocks.at[level, pl.ds(piece * chunk, chunk)],
            dst_ref=blocks.at[level, pl.ds(piece * chunk, chunk)],
            send_sem=block_send.at[level, position, piece],
            recv_sem=block_recv.at[level, piece],
            device_id=flipped(1 << position),
            device_id_type=MESH,
        )

    moves = []

    def block_start(level, position, piece):
        moves.append((level, position, piece))

        @pl.when(sends(level, position))
        def _():
            block_copy(level, position, piece).start()

    def block_wait(level, position, piece):
        @pl.when(receives(level, position))
        def _():
            block_copy(level, position, piece).wait_recv()

    def relay(phase):
        for piece in range(CHUNKS):
            for level in range(phase, depth):
                position = level - phase
                if phase > 1:
                    block_wait(level, position + 1, piece)
                block_start(level, position, piece)
        if phase == 1:
            for piece in range(CHUNKS):
                block_start(0, depth - 1, piece)
                block_start(depth, depth - 1, piece)
        if phase == 2:
            for piece in range(CHUNKS):
                block_wait(0, depth - 1, piece)
                block_wait(depth, depth - 1, piece)

            @pl.when(lax.rem(me, devices // 2) == 0)
            def _():
                blocks[depth + 1] = apply_transpose(blocks[0], blocks[depth])

            for piece in range(CHUNKS):
                block_start(depth + 1, depth - 2, piece)
        if phase > 2:
            for piece in range(CHUNKS):
                position = depth - phase
                block_wait(depth + 1, position + 1, piece)
                block_start(depth + 1, position, piece)

    def rows_at(level):
        return total_rows // 2 ** min(level, sharded)

    def span(side, size):
        return pl.ds(pl.multiple_of(side * size, size), size)

    def up_copy(level):
        if level <= sharded:
            source = skeletons[level - 1].at[span(1 - bit(level - 1), rows_at(level))]
        else:
            source = skeletons[level - 1]
        return pltpu.make_async_remote_copy(
            src_ref=source,
            dst_ref=arrived[level],
            send_sem=up_send.at[level],
            recv_sem=up_recv.at[level],
            device_id=flipped(1 << (level - 1)),
            device_id_type=MESH,
        )

    def joined(level):
        if level <= sharded:
            own = skeletons[level - 1][span(bit(level - 1), rows_at(level)), :]
        else:
            own = skeletons[level - 1][...]
        other = arrived[level][...]
        left = bit(level - 1) == 0
        return jnp.concatenate(
            [jnp.where(left, own, other), jnp.where(left, other, own)], axis=1
        )

    def down_copy(level):
        size = rows_at(level)
        return pltpu.make_async_remote_copy(
            src_ref=outgoing[level],
            dst_ref=known_rows[level - 1].at[span(bit(level - 1), size)],
            send_sem=down_send.at[level],
            recv_sem=down_recv.at[level],
            device_id=flipped(1 << (level - 1)),
            device_id_type=MESH,
        )

    load_node.wait()
    pl.semaphore_wait(barrier, len(deltas))
    relay(1)
    load_leaf.wait()
    load_rhs.wait()
    first = span(1 - bit(0), total_rows // 2)
    second = span(bit(0), total_rows // 2)
    skeletons[0][first, :] = apply_block(rhs[first, :], leaf[half:, :])
    up_copy(1).start()
    skeletons[0][second, :] = apply_block(rhs[second, :], leaf[half:, :])
    relay(2)
    leaf_e[...] = apply_block(rhs[...], leaf[:half, :])

    for level in range(1, depth):
        if level > 1:
            relay(level + 1)
        for piece in range(CHUNKS):
            block_wait(level, 0, piece)
        up_copy(level).wait_recv()
        merged = apply_block(joined(level), blocks[level])
        skeletons[level][...] = merged[:, half:]
        up_copy(level + 1).start()
        stored[level][...] = merged[:, :half]

    for piece in range(CHUNKS):
        block_wait(depth + 1, 0, piece)
    up_copy(depth).wait_recv()
    known = apply_block(joined(depth), blocks[depth + 1, span(bit(depth - 1), half), :])
    for level in range(depth - 1, sharded, -1):
        known = apply_transpose(
            jnp.concatenate([stored[level][...], known], axis=1),
            blocks[level, :, span(bit(level - 1), half)],
        )
    for level in range(sharded, 0, -1):
        if level < sharded:
            down_copy(level + 1).wait_recv()
            known = known_rows[level][...]
        expanded = apply_transpose(
            jnp.concatenate([stored[level][...], known], axis=1), blocks[level]
        )
        left = bit(level - 1) == 0
        outgoing[level][...] = jnp.where(left, expanded[:, half:], expanded[:, :half])
        down_copy(level).start()
        known_rows[level - 1][span(bit(level - 1), rows_at(level)), :] = jnp.where(
            left, expanded[:, :half], expanded[:, half:]
        )

    ones = jnp.ones((8, width), jnp.bfloat16)
    store_out = []
    load_diag.wait()
    totals = []
    for index, rows in enumerate((second, first)):
        if index == 1:
            down_copy(1).wait_recv()
        result = apply_transpose(
            jnp.concatenate([leaf_e[rows, :], known_rows[0][rows, :]], axis=1), leaf[...]
        )
        solved[rows, :] = result
        store = pltpu.make_async_copy(solved.at[rows], out_hbm.at[rows], local.at[4 + index])
        store.start()
        store_out.append(store)
        residual = rhs[rows, :] - apply_block(result, diag[...])
        high, low = halves(residual * residual)
        dims = (((1,), (1,)), ((), ()))
        totals.append(
            lax.dot_general(ones, high, dims, preferred_element_type=jnp.float32)
            + lax.dot_general(ones, low, dims, preferred_element_type=jnp.float32)
        )
    is_even = bit(0) == 0
    total = jnp.concatenate(
        [jnp.where(is_even, totals[0], totals[1]), jnp.where(is_even, totals[1], totals[0])], axis=1
    )[:1]

    def sum_copy(group, delta):
        position, size = groups[group]
        mine = lax.rem(lax.div(me, 2**position), 2**size)
        return pltpu.make_async_remote_copy(
            src_ref=sums.at[group],
            dst_ref=parts.at[group, mine],
            send_sem=sum_send.at[group, delta],
            recv_sem=sum_recv.at[group, delta],
            device_id=flipped(delta << position),
            device_id_type=MESH,
        )

    for group, (position, size) in enumerate(groups):
        mine = lax.rem(lax.div(me, 2**position), 2**size)
        sums[group] = total
        for delta in range(1, 2**size):
            sum_copy(group, delta).start()
        parts[group, mine] = total
        for delta in range(1, 2**size):
            sum_copy(group, delta).wait_recv()
        total = parts[group, 0]
        for member in range(1, 2**size):
            total = total + parts[group, member]
    norm_ref[...] = jnp.sqrt(total / (devices * width) + 1e-06)

    for level, position, piece in moves:

        @pl.when(sends(level, position))
        def _(level=level, position=position, piece=piece):
            block_copy(level, position, piece).wait_send()

    for level in range(1, depth + 1):
        up_copy(level).wait_send()
    for level in range(1, sharded + 1):
        down_copy(level).wait_send()
    for group, delta, _ in deltas:
        sum_copy(group, delta).wait_send()
    for store in store_out:
        store.wait()


def body(right_side, leaf_inverse, leaf_diag, node_block):
    columns = lax.axis_size("col")
    devices = lax.axis_size("row") * columns
    depth = devices.bit_length() - 1
    rows, width = right_side.shape
    half = width // 2
    sharded = 1
    while sharded < depth - 1 and sharded < 3 and rows % (2 ** (sharded + 1) * 16) == 0:
        sharded += 1
    groups = -(-depth // GROUP_BITS)

    def rows_at(level):
        return rows // 2 ** min(level, sharded)

    def vmem(*shape):
        return pltpu.VMEM(shape, jnp.float32)

    dma = pltpu.SemaphoreType.DMA
    scratch = [
        vmem(rows, width),
        vmem(width, width),
        vmem(width, width),
        vmem(rows, width),
        vmem(depth + 2, width, width),
        vmem(rows, half),
        vmem(groups, 2**GROUP_BITS, 1, rows),
        vmem(groups, 1, rows),
    ]
    scratch += [vmem(rows_at(level), half) for level in range(depth)]
    scratch += [vmem(rows_at(level), half) for level in range(1, depth + 1)]
    scratch += [vmem(rows_at(level), half) for level in range(1, depth)]
    scratch += [vmem(rows_at(level), half) for level in range(sharded)]
    scratch += [vmem(rows_at(level), half) for level in range(1, sharded + 1)]
    scratch += [
        dma((6,)),
        dma((depth + 2, depth, CHUNKS)),
        dma((depth + 2, CHUNKS)),
        dma((depth + 1,)),
        dma((depth + 1,)),
        dma((sharded + 1,)),
        dma((sharded + 1,)),
        dma((groups, 2**GROUP_BITS)),
        dma((groups, 2**GROUP_BITS)),
    ]
    anywhere = pl.BlockSpec(memory_space=pl.ANY)
    solved, norm = pl.pallas_call(
        functools.partial(kernel, devices, columns, sharded),
        out_shape=(
            jax.ShapeDtypeStruct((rows, width), jnp.float32),
            jax.ShapeDtypeStruct((1, rows), jnp.float32),
        ),
        in_specs=[anywhere] * 4,
        out_specs=(anywhere, pl.BlockSpec(memory_space=pltpu.VMEM)),
        scratch_shapes=scratch,
        compiler_params=pltpu.CompilerParams(collective_id=0, has_side_effects=True),
    )(right_side, leaf_inverse, leaf_diag, node_block)
    return (solved, norm.reshape(rows))


def solution(mesh):
    return jax.shard_map(
        body,
        mesh=mesh,
        in_specs=(
            P(None, ("row", "col")),
            P(("row", "col"), None, None),
            P(("row", "col"), None, None),
            P(("row", "col"), None, None),
        ),
        out_specs=(P(None, ("row", "col")), P()),
        check_vma=False,
    )
```

```python
import functools

import jax
import jax.numpy as jnp
from jax import lax
from jax.experimental import pallas as pl
from jax.experimental.pallas import tpu as pltpu
from jax.sharding import PartitionSpec as P

MESH = pl.DeviceIdType.MESH
PIECES = 1
GROUP_BITS = 5
STREAMS = 1
SHARDED = 1


def halves(value):
    high = value.astype(jnp.bfloat16)
    low = (value - high.astype(jnp.float32)).astype(jnp.bfloat16)
    return high, low


def product(vectors, block, contract):
    rows = vectors.shape[0]
    high, low = halves(vectors)
    block_high, block_low = block
    dims = (((1,), (contract,)), ((), ()))
    both = lax.dot_general(
        jnp.concatenate([high, low], axis=0), block_high, dims, preferred_element_type=jnp.float32
    )
    cross = lax.dot_general(high, block_low, dims, preferred_element_type=jnp.float32)
    return both[:rows] + (both[rows:] + cross)


def apply_block(vectors, block):
    return product(vectors, halves(block), 1)


def apply_transpose(vectors, block):
    return product(vectors, halves(block), 0)


def kernel(devices, columns, sharded, *refs):
    depth = devices.bit_length() - 1
    (rhs_hbm, leaf_hbm, diag_hbm, node_hbm, solved, norm_ref) = refs[:6]
    (rhs, leaf, diag, blocks, leaf_e, parts, sums) = refs[6:13]
    rest = list(refs[13:])
    skeletons = [rest.pop(0) for _ in range(depth)]
    arrived = [None] + [rest.pop(0) for _ in range(depth)]
    stored = [None] + [rest.pop(0) for _ in range(depth - 1)]
    known_rows = [rest.pop(0) for _ in range(sharded)]
    outgoing = [None] + [rest.pop(0) for _ in range(sharded)]
    (local, block_send, block_recv, up_send, up_recv, down_send, down_recv, sum_send, sum_recv) = rest

    total_rows, width = rhs.shape
    half = width // 2
    chunk = half // PIECES
    upper, lower = range(PIECES), range(PIECES, 2 * PIECES)
    me = lax.axis_index("row") * columns + lax.axis_index("col")

    def bit(position):
        return lax.rem(lax.div(me, 2**position), 2)

    def place(index):
        return (lax.div(index, columns), lax.rem(index, columns))

    def flipped(delta):
        other = me
        for position in range(depth):
            if delta >> position & 1:
                other = other + (1 - 2 * bit(position)) * 2**position
        return place(other)

    groups = []
    for first in range(0, depth, GROUP_BITS):
        groups.append((first, min(GROUP_BITS, depth - first)))
    deltas = [(g, d, d << first) for g, (first, size) in enumerate(groups) for d in range(1, 2**size)]

    slot = jnp.int32(0)
    for position in range(depth):
        slot = jnp.where(lax.rem(me, 2 ** (position + 1)) == 2**position, position + 1, slot)
    load_node = pltpu.make_async_copy(node_hbm.at[0], blocks.at[slot], local.at[0])
    load_leaf = pltpu.make_async_copy(leaf_hbm.at[0], leaf, local.at[1])
    load_rhs = pltpu.make_async_copy(rhs_hbm, rhs, local.at[2])
    load_diag = pltpu.make_async_copy(diag_hbm.at[0], diag, local.at[3])
    load_node.start()
    load_leaf.start()
    load_rhs.start()
    load_diag.start()

    barrier = pltpu.get_barrier_semaphore()
    for position in range(depth):
        pl.semaphore_signal(
            barrier, inc=1, device_id=flipped(1 << position), device_id_type=MESH
        )

    def sends(level, position):
        if level == 0:
            return me == 0
        if position == level - 1:
            return lax.rem(me, 2**level) == 2 ** (level - 1)
        return lax.rem(me, 2 ** (position + 1)) == 0

    def receives(level, position):
        if level == 0:
            return me == devices // 2
        if position == level - 1:
            return lax.rem(me, 2**level) == 0
        return lax.rem(me, 2 ** (position + 1)) == 2**position

    def block_copy(level, position, piece):
        rows = pl.ds(piece * chunk, chunk)
        return pltpu.make_async_remote_copy(
            src_ref=blocks.at[level, rows],
            dst_ref=blocks.at[level, rows],
            send_sem=block_send.at[level, position, piece],
            recv_sem=block_recv.at[level, piece],
            device_id=flipped(1 << position),
            device_id_type=MESH,
        )

    moves = []

    def block_start(level, position, piece):
        moves.append((level, position, piece))

        @pl.when(sends(level, position))
        def _():
            block_copy(level, position, piece).start()

    def block_wait(level, position, piece):
        @pl.when(receives(level, position))
        def _():
            block_copy(level, position, piece).wait_recv()

    def relay(phase, pieces):
        for piece in pieces:
            for level in range(phase, depth):
                position = level - phase
                if phase > 1:
                    block_wait(level, position + 1, piece)
                block_start(level, position, piece)

    def relay_root(phase):
        if phase == 1:
            for piece in (*upper, *lower):
                block_start(depth, depth - 1, piece)
            for piece in lower:
                block_start(0, depth - 1, piece)
            return
        if phase == 2:
            for piece in (*upper, *lower):
                block_wait(depth, depth - 1, piece)
            for piece in lower:
                block_wait(0, depth - 1, piece)

            @pl.when(lax.rem(me, devices // 2) == 0)
            def _():
                blocks[depth + 1, :half] = apply_transpose(
                    blocks[0, span(bit(depth - 1), half)], blocks[depth]
                )

        for piece in upper:
            position = depth - phase
            if phase > 2:
                block_wait(depth + 1, position + 1, piece)
            block_start(depth + 1, position, piece)

    def rows_at(level):
        return total_rows // 2 ** min(level, sharded)

    def span(side, size):
        return pl.ds(pl.multiple_of(side * size, size), size)

    def stream(level, index, side=None):
        size = rows_at(level) // STREAMS
        if side is None:
            return pl.ds(index * size, size)
        return pl.ds(pl.multiple_of(side * rows_at(level) + index * size, 8), size)

    def side_of(level):
        return bit(level - 1) if level <= sharded else None

    def other_side(level):
        return 1 - bit(level - 1) if level <= sharded else None

    def up_copy(level, index):
        return pltpu.make_async_remote_copy(
            src_ref=skeletons[level - 1].at[stream(level, index, other_side(level))],
            dst_ref=arrived[level].at[stream(level, index)],
            send_sem=up_send.at[level, index],
            recv_sem=up_recv.at[level, index],
            device_id=flipped(1 << (level - 1)),
            device_id_type=MESH,
        )

    def joined(level, index):
        own = skeletons[level - 1][stream(level, index, side_of(level)), :]
        other = arrived[level][stream(level, index), :]
        left = bit(level - 1) == 0
        return jnp.concatenate(
            [jnp.where(left, own, other), jnp.where(left, other, own)], axis=1
        )

    def down_copy(level, index):
        return pltpu.make_async_remote_copy(
            src_ref=outgoing[level].at[stream(level, index)],
            dst_ref=known_rows[level - 1].at[stream(level, index, bit(level - 1))],
            send_sem=down_send.at[level, index],
            recv_sem=down_recv.at[level, index],
            device_id=flipped(1 << (level - 1)),
            device_id_type=MESH,
        )

    load_node.wait()
    pl.semaphore_wait(barrier, depth)
    relay(1, lower)
    relay_root(1)
    load_leaf.wait()
    load_rhs.wait()
    lift = halves(leaf[half:, :])
    for index in range(STREAMS):
        rows = stream(1, index, other_side(1))
        skeletons[0][rows, :] = product(rhs[rows, :], lift, 1)
        up_copy(1, index).start()
    for index in range(STREAMS):
        rows = stream(1, index, side_of(1))
        skeletons[0][rows, :] = product(rhs[rows, :], lift, 1)
    leaf_e[...] = apply_block(rhs[...], leaf[:half, :])

    def keep(level):
        for piece in upper:
            block_wait(level, 0, piece)
        weights = halves(blocks[level, :half])
        for index in range(STREAMS):
            stored[level][stream(level, index), :] = product(joined(level, index), weights, 1)

    for level in range(1, depth):
        for piece in lower:
            block_wait(level, 0, piece)
        weights = halves(blocks[level, half:])
        for index in range(STREAMS):
            up_copy(level, index).wait_recv()
            result = product(joined(level, index), weights, 1)
            skeletons[level][stream(level, index), :] = result
            if level >= sharded:
                up_copy(level + 1, index).start()
        if level < sharded:
            for index in range(STREAMS):
                up_copy(level + 1, index).start()
        relay(level + 1, lower)
        relay(level, upper)
        relay_root(level + 1)
        if level > 1:
            keep(level - 1)
    keep(depth - 1)

    for piece in upper:
        block_wait(depth + 1, 0, piece)
    root_weights = halves(blocks[depth + 1, :half])
    above = {
        level: halves(blocks[level, :, span(bit(level - 1), half)])
        for level in range(depth - 1, sharded, -1)
    }

    def lower_rows(level, index, known, weights):
        joint = jnp.concatenate([stored[level][stream(level, index), :], known], axis=1)
        expanded = product(joint, weights, 0)
        left = bit(level - 1) == 0
        outgoing[level][stream(level, index), :] = jnp.where(
            left, expanded[:, half:], expanded[:, :half]
        )
        down_copy(level, index).start()
        known_rows[level - 1][stream(level, index, bit(level - 1)), :] = jnp.where(
            left, expanded[:, :half], expanded[:, half:]
        )

    weights = halves(blocks[sharded])
    for index in range(STREAMS):
        up_copy(depth, index).wait_recv()
        known = product(joined(depth, index), root_weights, 1)
        for level in range(depth - 1, sharded, -1):
            joint = jnp.concatenate([stored[level][stream(level, index), :], known], axis=1)
            known = product(joint, above[level], 0)
        lower_rows(sharded, index, known, weights)
    for level in range(sharded - 1, 0, -1):
        weights = halves(blocks[level])
        for index in range(STREAMS):
            down_copy(level + 1, index).wait_recv()
        for index in range(STREAMS):
            lower_rows(level, index, known_rows[level][stream(level, index), :], weights)

    ones = jnp.ones((8, width), jnp.bfloat16)
    load_diag.wait()
    leaf_weights = halves(leaf[...])
    diag_weights = halves(diag[...])
    totals = []
    for mine in (True, False):
        squares = []
        for index in range(STREAMS):
            rows = stream(1, index, side_of(1) if mine else other_side(1))
            if not mine:
                down_copy(1, index).wait_recv()
            joint = jnp.concatenate([leaf_e[rows, :], known_rows[0][rows, :]], axis=1)
            result = product(joint, leaf_weights, 0)
            solved[rows, :] = result
            residual = rhs[rows, :] - product(result, diag_weights, 1)
            squares.append(residual * residual)
        high, low = halves(jnp.concatenate(squares, axis=0))
        dims = (((1,), (1,)), ((), ()))
        totals.append(
            lax.dot_general(ones, high, dims, preferred_element_type=jnp.float32)
            + lax.dot_general(ones, low, dims, preferred_element_type=jnp.float32)
        )
    is_even = bit(0) == 0
    total = jnp.concatenate(
        [jnp.where(is_even, totals[0], totals[1]), jnp.where(is_even, totals[1], totals[0])], axis=1
    )[:1]

    def sum_copy(group, delta):
        position, size = groups[group]
        mine = lax.rem(lax.div(me, 2**position), 2**size)
        return pltpu.make_async_remote_copy(
            src_ref=sums.at[group],
            dst_ref=parts.at[group, mine],
            send_sem=sum_send.at[group, delta],
            recv_sem=sum_recv.at[group, delta],
            device_id=flipped(delta << position),
            device_id_type=MESH,
        )

    for group, (position, size) in enumerate(groups):
        mine = lax.rem(lax.div(me, 2**position), 2**size)
        sums[group] = total
        for delta in range(1, 2**size):
            sum_copy(group, delta).start()
        parts[group, mine] = total
        for delta in range(1, 2**size):
            sum_copy(group, delta).wait_recv()
        total = parts[group, 0]
        for member in range(1, 2**size):
            total = total + parts[group, member]
    norm_ref[...] = jnp.sqrt(total / (devices * width) + 1e-06).reshape(total_rows)

    for level, position, piece in moves:

        @pl.when(sends(level, position))
        def _(level=level, position=position, piece=piece):
            block_copy(level, position, piece).wait_send()

    for level in range(1, depth + 1):
        for index in range(STREAMS):
            up_copy(level, index).wait_send()
    for level in range(1, sharded + 1):
        for index in range(STREAMS):
            down_copy(level, index).wait_send()
    for group, delta, _ in deltas:
        sum_copy(group, delta).wait_send()


def body(right_side, leaf_inverse, leaf_diag, node_block):
    columns = lax.axis_size("col")
    devices = lax.axis_size("row") * columns
    depth = devices.bit_length() - 1
    rows, width = right_side.shape
    half = width // 2
    sharded = 1
    while sharded < depth - 1 and sharded < SHARDED and rows % (2 ** (sharded + 1) * 16 * STREAMS) == 0:
        sharded += 1
    groups = -(-depth // GROUP_BITS)

    def rows_at(level):
        return rows // 2 ** min(level, sharded)

    def vmem(*shape):
        return pltpu.VMEM(shape, jnp.float32)

    dma = pltpu.SemaphoreType.DMA
    scratch = [
        vmem(rows, width),
        vmem(width, width),
        vmem(width, width),
        vmem(depth + 2, width, width),
        vmem(rows, half),
        vmem(groups, 2**GROUP_BITS, 1, rows),
        vmem(groups, 1, rows),
    ]
    scratch += [vmem(rows_at(level), half) for level in range(depth)]
    scratch += [vmem(rows_at(level), half) for level in range(1, depth + 1)]
    scratch += [vmem(rows_at(level), half) for level in range(1, depth)]
    scratch += [vmem(rows_at(level), half) for level in range(sharded)]
    scratch += [vmem(rows_at(level), half) for level in range(1, sharded + 1)]
    scratch += [
        dma((4,)),
        dma((depth + 2, depth, 2 * PIECES)),
        dma((depth + 2, 2 * PIECES)),
        dma((depth + 1, STREAMS)),
        dma((depth + 1, STREAMS)),
        dma((sharded + 1, STREAMS)),
        dma((sharded + 1, STREAMS)),
        dma((groups, 2**GROUP_BITS)),
        dma((groups, 2**GROUP_BITS)),
    ]
    in_hbm = pl.BlockSpec(memory_space=pltpu.HBM)
    in_vmem = pl.BlockSpec(memory_space=pltpu.VMEM)
    arguments = [
        pltpu.with_memory_space_constraint(argument, pltpu.HBM)
        for argument in (right_side, leaf_inverse, leaf_diag, node_block)
    ]
    solved, norm = pl.pallas_call(
        functools.partial(kernel, devices, columns, sharded),
        out_shape=(
            pltpu.VMEM((rows, width), jnp.float32),
            jax.ShapeDtypeStruct((rows,), jnp.float32),
        ),
        in_specs=[in_hbm] * 4,
        out_specs=(in_vmem, in_vmem),
        scratch_shapes=scratch,
        compiler_params=pltpu.CompilerParams(vmem_limit_bytes=16 * 2**20, collective_id=0, has_side_effects=True),
    )(*arguments)
    return (solved, norm)


def solution(mesh):
    return jax.shard_map(
        body,
        mesh=mesh,
        in_specs=(
            P(None, ("row", "col")),
            P(("row", "col"), None, None),
            P(("row", "col"), None, None),
            P(("row", "col"), None, None),
        ),
        out_specs=(P(None, ("row", "col")), P()),
        check_vma=False,
    )
```

```python
import functools

import jax
import jax.numpy as jnp
from jax import lax
from jax.experimental import pallas as pl
from jax.experimental.pallas import tpu as pltpu
from jax.sharding import PartitionSpec as P

MESH = pl.DeviceIdType.MESH
PIECES = 1
GROUP_BITS = 5
STREAMS = 1
SHARDED = 1
TREES = {}


def halves(value):
    high = value.astype(jnp.bfloat16)
    low = (value - high.astype(jnp.float32)).astype(jnp.bfloat16)
    return high, low


def product(vectors, block, contract):
    rows = vectors.shape[0]
    high, low = halves(vectors)
    block_high, block_low = block
    dims = (((1,), (contract,)), ((), ()))
    both = lax.dot_general(
        jnp.concatenate([high, low], axis=0), block_high, dims, preferred_element_type=jnp.float32
    )
    cross = lax.dot_general(high, block_low, dims, preferred_element_type=jnp.float32)
    return both[:rows] + (both[rows:] + cross)


def apply_block(vectors, block):
    return product(vectors, halves(block), 1)


def apply_transpose(vectors, block):
    return product(vectors, halves(block), 0)


def kernel(devices, columns, sharded, *refs):
    depth = devices.bit_length() - 1
    (rhs_hbm, leaf_hbm, diag_hbm, node_hbm, solved, norm_ref) = refs[:6]
    (rhs, leaf, diag, blocks, leaf_e, parts, sums) = refs[6:13]
    rest = list(refs[13:])
    skeletons = [rest.pop(0) for _ in range(depth)]
    arrived = [None] + [rest.pop(0) for _ in range(depth)]
    stored = [None] + [rest.pop(0) for _ in range(depth - 1)]
    known_rows = [rest.pop(0) for _ in range(sharded)]
    outgoing = [None] + [rest.pop(0) for _ in range(sharded)]
    (local, block_send, block_recv, up_send, up_recv, down_send, down_recv, sum_send, sum_recv) = rest

    total_rows, width = rhs.shape
    half = width // 2
    chunk = half // PIECES
    upper, lower = range(PIECES), range(PIECES, 2 * PIECES)
    me = lax.axis_index("row") * columns + lax.axis_index("col")

    bits = [lax.rem(lax.div(me, 2**position), 2) for position in range(depth)]

    def bit(position):
        return bits[position]

    def place(index):
        return (lax.div(index, columns), lax.rem(index, columns))

    def flip(delta):
        other = me
        for position in range(depth):
            if delta >> position & 1:
                other = other + (1 - 2 * bit(position)) * 2**position
        return place(other)

    groups = []
    for first in range(0, depth, GROUP_BITS):
        groups.append((first, min(GROUP_BITS, depth - first)))
    deltas = [(g, d, d << first) for g, (first, size) in enumerate(groups) for d in range(1, 2**size)]

    partners = {delta: flip(delta) for _, _, delta in deltas}

    def flipped(delta):
        return partners[delta]

    slot = jnp.int32(0)
    for position in range(depth):
        slot = jnp.where(lax.rem(me, 2 ** (position + 1)) == 2**position, position + 1, slot)
    load_node = pltpu.make_async_copy(node_hbm.at[0], blocks.at[slot], local.at[0])
    load_leaf = pltpu.make_async_copy(leaf_hbm.at[0], leaf, local.at[1])
    load_rhs = pltpu.make_async_copy(rhs_hbm, rhs, local.at[2])
    load_diag = pltpu.make_async_copy(diag_hbm.at[0], diag, local.at[3])
    load_node.start()
    load_leaf.start()
    load_rhs.start()
    load_diag.start()

    barrier = pltpu.get_barrier_semaphore()
    for position in range(depth):
        pl.semaphore_signal(
            barrier, inc=1, device_id=flipped(1 << position), device_id_type=MESH
        )

    orders = {0: [depth - 1], depth: [depth - 1], depth + 1: list(range(depth - 2, -1, -1))}
    for level in range(1, depth):
        orders[level] = list(range(level - 1, -1, -1))
    for level, order in TREES.items():
        if level < depth:
            orders[level] = list(order)

    def match(level, phase, moved):
        held = jnp.int32(0)
        for place_in_order, position in enumerate(orders[level]):
            if place_in_order >= phase:
                owner = int(0 < level <= depth and position == level - 1)
                if moved and place_in_order == phase:
                    owner = 1 - owner
                here = bit(position)
                held = held + (here if owner == 0 else 1 - here)
        if level in (0, depth):
            held = held + lax.rem(me, devices // 2)
        return held == 0

    match_of = {
        (level, phase, moved): match(level, phase, moved)
        for level in orders
        for phase in range(len(orders[level]))
        for moved in (False, True)
    }

    def matches(level, phase, moved):
        return match_of[level, phase, moved]

    def block_copy(level, phase, piece):
        rows = pl.ds(piece * chunk, chunk)
        return pltpu.make_async_remote_copy(
            src_ref=blocks.at[level, rows],
            dst_ref=blocks.at[level, rows],
            send_sem=block_send.at[level, phase, piece],
            recv_sem=block_recv.at[level, piece],
            device_id=flipped(1 << orders[level][phase]),
            device_id_type=MESH,
        )

    moves = []

    def block_start(level, phase, piece):
        moves.append((level, phase, piece))

        @pl.when(matches(level, phase, False))
        def _():
            block_copy(level, phase, piece).start()

    def block_wait(level, phase, piece):
        @pl.when(matches(level, phase, True))
        def _():
            block_copy(level, phase, piece).wait_recv()

    def last_wait(level, piece):
        block_wait(level, len(orders[level]) - 1, piece)

    def relay(phase, pieces):
        for piece in pieces:
            for level in range(phase, depth):
                if phase > 1:
                    block_wait(level, phase - 2, piece)
                block_start(level, phase - 1, piece)

    def relay_root(phase):
        if phase == 1:
            for piece in (*upper, *lower):
                block_start(depth, 0, piece)
            for piece in lower:
                block_start(0, 0, piece)
            return
        if phase == 2:
            for piece in (*upper, *lower):
                block_wait(depth, 0, piece)
            for piece in lower:
                block_wait(0, 0, piece)

            @pl.when(lax.rem(me, devices // 2) == 0)
            def _():
                blocks[depth + 1, :half] = apply_transpose(
                    blocks[0, span(bit(depth - 1), half)], blocks[depth]
                )

        for piece in upper:
            if phase > 2:
                block_wait(depth + 1, phase - 3, piece)
            block_start(depth + 1, phase - 2, piece)

    def rows_at(level):
        return total_rows // 2 ** min(level, sharded)

    def span(side, size):
        return pl.ds(pl.multiple_of(side * size, size), size)

    def stream(level, index, side=None):
        size = rows_at(level) // STREAMS
        if side is None:
            return pl.ds(index * size, size)
        return pl.ds(pl.multiple_of(side * rows_at(level) + index * size, 8), size)

    def side_of(level):
        return bit(level - 1) if level <= sharded else None

    def other_side(level):
        return 1 - bit(level - 1) if level <= sharded else None

    def up_copy(level, index):
        return pltpu.make_async_remote_copy(
            src_ref=skeletons[level - 1].at[stream(level, index, other_side(level))],
            dst_ref=arrived[level].at[stream(level, index)],
            send_sem=up_send.at[level, index],
            recv_sem=up_recv.at[level, index],
            device_id=flipped(1 << (level - 1)),
            device_id_type=MESH,
        )

    def joined(level, index):
        own = skeletons[level - 1][stream(level, index, side_of(level)), :]
        other = arrived[level][stream(level, index), :]
        left = bit(level - 1) == 0
        return jnp.concatenate(
            [jnp.where(left, own, other), jnp.where(left, other, own)], axis=1
        )

    def down_copy(level, index):
        return pltpu.make_async_remote_copy(
            src_ref=outgoing[level].at[stream(level, index)],
            dst_ref=known_rows[level - 1].at[stream(level, index, bit(level - 1))],
            send_sem=down_send.at[level, index],
            recv_sem=down_recv.at[level, index],
            device_id=flipped(1 << (level - 1)),
            device_id_type=MESH,
        )

    load_node.wait()
    pl.semaphore_wait(barrier, depth)
    relay(1, lower)
    relay_root(1)
    load_leaf.wait()
    load_rhs.wait()
    lift = halves(leaf[half:, :])
    for index in range(STREAMS):
        rows = stream(1, index, other_side(1))
        skeletons[0][rows, :] = product(rhs[rows, :], lift, 1)
        up_copy(1, index).start()
    for index in range(STREAMS):
        rows = stream(1, index, side_of(1))
        skeletons[0][rows, :] = product(rhs[rows, :], lift, 1)
    leaf_e[...] = apply_block(rhs[...], leaf[:half, :])

    def keep(level):
        for piece in upper:
            last_wait(level, piece)
        weights = halves(blocks[level, :half])
        for index in range(STREAMS):
            stored[level][stream(level, index), :] = product(joined(level, index), weights, 1)

    for level in range(1, depth):
        for piece in lower:
            last_wait(level, piece)
        weights = halves(blocks[level, half:])
        for index in range(STREAMS):
            up_copy(level, index).wait_recv()
            result = product(joined(level, index), weights, 1)
            skeletons[level][stream(level, index), :] = result
            if level >= sharded:
                up_copy(level + 1, index).start()
        if level < sharded:
            for index in range(STREAMS):
                up_copy(level + 1, index).start()
        relay(level + 1, lower)
        relay(level, upper)
        relay_root(level + 1)
        if level > 1:
            keep(level - 1)
    keep(depth - 1)

    for piece in upper:
        last_wait(depth + 1, piece)
    root_weights = halves(blocks[depth + 1, :half])
    above = {
        level: halves(blocks[level, :, span(bit(level - 1), half)])
        for level in range(depth - 1, sharded, -1)
    }

    def lower_rows(level, index, known, weights):
        joint = jnp.concatenate([stored[level][stream(level, index), :], known], axis=1)
        expanded = product(joint, weights, 0)
        left = bit(level - 1) == 0
        outgoing[level][stream(level, index), :] = jnp.where(
            left, expanded[:, half:], expanded[:, :half]
        )
        down_copy(level, index).start()
        known_rows[level - 1][stream(level, index, bit(level - 1)), :] = jnp.where(
            left, expanded[:, :half], expanded[:, half:]
        )

    weights = halves(blocks[sharded])
    for index in range(STREAMS):
        up_copy(depth, index).wait_recv()
        known = product(joined(depth, index), root_weights, 1)
        for level in range(depth - 1, sharded, -1):
            joint = jnp.concatenate([stored[level][stream(level, index), :], known], axis=1)
            known = product(joint, above[level], 0)
        lower_rows(sharded, index, known, weights)
    for level in range(sharded - 1, 0, -1):
        weights = halves(blocks[level])
        for index in range(STREAMS):
            down_copy(level + 1, index).wait_recv()
        for index in range(STREAMS):
            lower_rows(level, index, known_rows[level][stream(level, index), :], weights)

    ones = jnp.ones((8, width), jnp.bfloat16)
    load_diag.wait()
    leaf_weights = halves(leaf[...])
    diag_weights = halves(diag[...])
    totals = []
    for mine in (True, False):
        squares = []
        for index in range(STREAMS):
            rows = stream(1, index, side_of(1) if mine else other_side(1))
            if not mine:
                down_copy(1, index).wait_recv()
            joint = jnp.concatenate([leaf_e[rows, :], known_rows[0][rows, :]], axis=1)
            result = product(joint, leaf_weights, 0)
            solved[rows, :] = result
            residual = rhs[rows, :] - product(result, diag_weights, 1)
            squares.append(residual * residual)
        high, low = halves(jnp.concatenate(squares, axis=0))
        dims = (((1,), (1,)), ((), ()))
        totals.append(
            lax.dot_general(ones, high, dims, preferred_element_type=jnp.float32)
            + lax.dot_general(ones, low, dims, preferred_element_type=jnp.float32)
        )
    is_even = bit(0) == 0
    total = jnp.concatenate(
        [jnp.where(is_even, totals[0], totals[1]), jnp.where(is_even, totals[1], totals[0])], axis=1
    )[:1]

    def sum_copy(group, delta):
        position, size = groups[group]
        mine = lax.rem(lax.div(me, 2**position), 2**size)
        return pltpu.make_async_remote_copy(
            src_ref=sums.at[group],
            dst_ref=parts.at[group, mine],
            send_sem=sum_send.at[group, delta],
            recv_sem=sum_recv.at[group, delta],
            device_id=flipped(delta << position),
            device_id_type=MESH,
        )

    def drain():
        for level, phase, piece in moves:

            @pl.when(matches(level, phase, False))
            def _(level=level, phase=phase, piece=piece):
                block_copy(level, phase, piece).wait_send()

        for level in range(1, depth + 1):
            for index in range(STREAMS):
                up_copy(level, index).wait_send()
        for level in range(1, sharded + 1):
            for index in range(STREAMS):
                down_copy(level, index).wait_send()

    for group, (position, size) in enumerate(groups):
        mine = lax.rem(lax.div(me, 2**position), 2**size)
        sums[group] = total
        for delta in reversed(range(1, 2**size)):
            sum_copy(group, delta).start()
        parts[group, mine] = total
        if group == 0:
            drain()
        for delta in range(1, 2**size):
            sum_copy(group, delta).wait_recv()
        total = parts[group, 0]
        for member in range(1, 2**size):
            total = total + parts[group, member]
    norm_ref[...] = jnp.sqrt(total / (devices * width) + 1e-06).reshape(total_rows)

    for group, delta, _ in deltas:
        sum_copy(group, delta).wait_send()


def body(right_side, leaf_inverse, leaf_diag, node_block):
    columns = lax.axis_size("col")
    devices = lax.axis_size("row") * columns
    depth = devices.bit_length() - 1
    rows, width = right_side.shape
    half = width // 2
    sharded = 1
    while sharded < depth - 1 and sharded < SHARDED and rows % (2 ** (sharded + 1) * 16 * STREAMS) == 0:
        sharded += 1
    groups = -(-depth // GROUP_BITS)

    def rows_at(level):
        return rows // 2 ** min(level, sharded)

    def vmem(*shape):
        return pltpu.VMEM(shape, jnp.float32)

    dma = pltpu.SemaphoreType.DMA
    scratch = [
        vmem(rows, width),
        vmem(width, width),
        vmem(width, width),
        vmem(depth + 2, width, width),
        vmem(rows, half),
        vmem(groups, 2**GROUP_BITS, 1, rows),
        vmem(groups, 1, rows),
    ]
    scratch += [vmem(rows_at(level), half) for level in range(depth)]
    scratch += [vmem(rows_at(level), half) for level in range(1, depth + 1)]
    scratch += [vmem(rows_at(level), half) for level in range(1, depth)]
    scratch += [vmem(rows_at(level), half) for level in range(sharded)]
    scratch += [vmem(rows_at(level), half) for level in range(1, sharded + 1)]
    scratch += [
        dma((4,)),
        dma((depth + 2, depth, 2 * PIECES)),
        dma((depth + 2, 2 * PIECES)),
        dma((depth + 1, STREAMS)),
        dma((depth + 1, STREAMS)),
        dma((sharded + 1, STREAMS)),
        dma((sharded + 1, STREAMS)),
        dma((groups, 2**GROUP_BITS)),
        dma((groups, 2**GROUP_BITS)),
    ]
    in_hbm = pl.BlockSpec(memory_space=pltpu.HBM)
    in_vmem = pl.BlockSpec(memory_space=pltpu.VMEM)
    arguments = [
        pltpu.with_memory_space_constraint(argument, pltpu.HBM)
        for argument in (right_side, leaf_inverse, leaf_diag, node_block)
    ]
    solved, norm = pl.pallas_call(
        functools.partial(kernel, devices, columns, sharded),
        out_shape=(
            pltpu.VMEM((rows, width), jnp.float32),
            jax.ShapeDtypeStruct((rows,), jnp.float32),
        ),
        in_specs=[in_hbm] * 4,
        out_specs=(in_vmem, in_vmem),
        scratch_shapes=scratch,
        compiler_params=pltpu.CompilerParams(vmem_limit_bytes=16 * 2**20, collective_id=0, has_side_effects=True),
    )(*arguments)
    return (solved, norm)


def solution(mesh):
    return jax.shard_map(
        body,
        mesh=mesh,
        in_specs=(
            P(None, ("row", "col")),
            P(("row", "col"), None, None),
            P(("row", "col"), None, None),
            P(("row", "col"), None, None),
        ),
        out_specs=(P(None, ("row", "col")), P()),
        check_vma=False,
    )
```
